512 devices in a mesh: field: 64 (over z, y), batch: 8 (over x, core).
Axes of the slice: x: 4, y: 8, z: 8, core: 2. Of those that a mesh axis runs over, the one named last changes fastest.
Arguments:
- pooled: bfloat16 [4096, 64, 1024], P('batch', 'field'), may hold values from -6 to 6
- counts: int32 [4096, 64], P('batch', 'field'), may hold values from 1 to 16
- w_pairs: bfloat16 [64, 504, 1024], P('field', None, 'batch'), may hold values from -0.03125 to 0.03125
- bias_terms: bfloat16 [1024], P('batch'), may hold values from -4 to 4
- grad_act: bfloat16 [4096, 1024], P('batch'), may hold values from -6 to 6
Outputs:
- entry_grad: bfloat16 [4096, 64, 1024], P('batch', 'field')
- weight_grad: float32 [64, 504, 1024], P('field', None, 'batch')
The draws below stay inside these ranges and needn't reach their ends.
All inputs are finite; a program needn't handle non-finite values.
Results may differ from the reference program's by a relative error of at most 0.014.
Values may be sent and summed in bfloat16 or wider, within the bound.
No kernel may reach another device: no remote copies, remote signals or barrier semaphores. Data moves between devices by JAX's collectives and lax.ppermute only.
A program may use at most 64 MiB of HBM per device.

```python
import jax
import jax.numpy as jnp
from jax import lax

B_DEV = 512
K = 16
H = 1024
FIELDS = 64
SAMPLES = 4096


def plant(values, key, low, largest):
    spot = [jax.random.randint(jax.random.fold_in(key, axis), (), 0, length) for axis, length in enumerate(values.shape)]
    widest = values.shape.index(max(values.shape))
    beside = spot[:widest] + [(spot[widest] + 1) % values.shape[widest]] + spot[widest + 1:]
    return values.at[tuple(spot)].set(low).at[tuple(beside)].set(largest)


def levels(own_key, extent, split, low, largest):
    loudness, own = 1.0, jax.random.fold_in(own_key, 6)
    for position, parts in split:
        draws = jnp.exp(jax.random.uniform(jax.random.fold_in(own, position), (parts,), jnp.float32, low / len(split), largest / len(split)))
        loudness = loudness * jnp.repeat(draws, extent[position] // parts).reshape([-1 if axis == position else 1 for axis in range(len(extent))])
    return loudness


def scatter_about(key, dims, deviation, limit, split=(), held_as=jnp.bfloat16):
    entries = jax.random.normal(key, dims, jnp.float32) * deviation
    if len(split) > 0:
        entries = levels(key, dims, split, -0.22, 0.18) * entries
    return jnp.clip(entries, min=-limit, max=limit).astype(held_as)


def setup_inputs(seed: int = 0) -> dict:
    splits = jax.random.split(jax.random.key(seed), 6)
    return {
        "pooled": scatter_about(splits[0], (SAMPLES, FIELDS, FIELDS * K), 1.0, 6.0, ((0, 8), (1, 64))),
        "counts": plant(jax.random.randint(splits[1], (SAMPLES, FIELDS), 1, 17), jax.random.fold_in(splits[1], 1), 1, 16).astype(jnp.int32),
        "w_pairs": scatter_about(splits[2], (FIELDS, (FIELDS - 1) * (K // 2), H), (FIELDS * (FIELDS - 1) * (K // 2)) ** -0.5, 0.03125, ((0, 64), (2, 8))),
        "bias_terms": scatter_about(splits[3], (H,), 1.0, 4.0, ((0, 8),)),
        "grad_act": scatter_about(splits[4], (SAMPLES, H), 1.0, 6.0, ((0, 8),)),
    }


def reference(pooled, counts, w_pairs, bias_terms, grad_act):
    half_depth = K // 2
    own_field = jnp.broadcast_to(jnp.arange(FIELDS, dtype=jnp.int32)[:, None], (FIELDS, FIELDS - 1))
    slot_index = jnp.broadcast_to(jnp.arange(FIELDS - 1, dtype=jnp.int32)[None, :], (FIELDS, FIELDS - 1))
    upper_half = slot_index < own_field
    partner = slot_index + (slot_index >= own_field).astype(jnp.int32)
    weights = w_pairs.astype(jnp.float32)
    bias_wide = bias_terms.astype(jnp.float32)
    sample_rows = B_DEV
    blocks_count = pooled.shape[0] // sample_rows

    def owned_half(tensor):
        picked = tensor[:, own_field, partner, :]
        return jnp.where(upper_half[None, :, :, None], picked[..., half_depth:], picked[..., :half_depth])

    def sample_block(weight_total, inputs):
        pooled_block, count_block, grad_block = inputs
        embedded = pooled_block.astype(jnp.float32).reshape(sample_rows, FIELDS, FIELDS, K)
        flipped = jnp.swapaxes(embedded, 1, 2)
        products = (owned_half(embedded) * owned_half(flipped)).astype(jnp.bfloat16)
        pair_rows = products.astype(jnp.float32).reshape(sample_rows, FIELDS, (FIELDS - 1) * half_depth)
        hidden = jnp.einsum('rip,iph->rh', pair_rows, weights) + bias_wide
        gate_value = jax.nn.sigmoid(hidden)
        slope_act = (grad_block.astype(jnp.float32) * gate_value * (1.0 + hidden * (1.0 - gate_value))).astype(jnp.bfloat16)
        slope_wide = slope_act.astype(jnp.float32)
        pair_grad = jnp.einsum('rh,iph->rip', slope_wide, weights).reshape(sample_rows, FIELDS, FIELDS - 1, half_depth)
        weight_total = weight_total + jnp.einsum('rip,rh->iph', pair_rows, slope_wide)
        zero_half = jnp.zeros_like(pair_grad)
        placed = jnp.where(upper_half[None, :, :, None], jnp.concatenate([zero_half, pair_grad], -1), jnp.concatenate([pair_grad, zero_half], -1))
        dense_grad = jnp.zeros((sample_rows, FIELDS, FIELDS, K), jnp.float32).at[:, own_field, partner, :].set(placed)
        local_part = dense_grad * flipped
        partner_part = lax.optimization_barrier((jnp.swapaxes(dense_grad, 1, 2) * flipped).astype(jnp.bfloat16))
        block_grad = local_part + partner_part.astype(jnp.float32)
        block_grad = block_grad / jnp.sqrt(count_block.astype(jnp.float32))[:, :, None, None]
        return (weight_total, block_grad.reshape(sample_rows, FIELDS, FIELDS * K).astype(jnp.bfloat16))
    weight_start = jnp.zeros((FIELDS, (FIELDS - 1) * half_depth, H), jnp.float32)
    stacked = (pooled.reshape(blocks_count, sample_rows, FIELDS, FIELDS * K), counts.reshape(blocks_count, sample_rows, FIELDS), grad_act.reshape(blocks_count, sample_rows, H))
    weight_total, entry_grads = lax.scan(sample_block, weight_start, stacked)
    return (entry_grads.reshape(pooled.shape[0], FIELDS, FIELDS * K), weight_total)
```

```python
import jax
import jax.numpy as jnp
from jax import lax
from jax.sharding import PartitionSpec as P


def body(pooled, counts, w_pairs, bias_terms, grad_act):
    sample_rows = pooled.shape[0]
    fields = lax.axis_size("field")
    shards = lax.axis_size("batch")
    depth = pooled.shape[2] // fields
    half_depth = depth // 2
    hidden_units = grad_act.shape[1]
    pair_count = w_pairs.shape[1]
    own_rows = sample_rows // fields
    my_field = lax.axis_index("field")
    f32, bf16 = jnp.float32, jnp.bfloat16

    embedded = pooled.reshape(sample_rows, fields, depth).transpose(1, 2, 0)
    partner = jnp.arange(fields, dtype=jnp.int32)[:, None, None]
    upper_half = partner < my_field
    mine = jnp.where(upper_half, embedded[:, half_depth:], embedded[:, :half_depth])
    outbound = jnp.where(upper_half, embedded[:, :half_depth], embedded[:, half_depth:])
    received = lax.all_to_all(outbound, "field", split_axis=0, concat_axis=0, tiled=True)

    bias_rows = jnp.pad(bias_terms[None, :], ((0, 0), (0, 0)))
    weight_bias = lax.all_gather(
        jnp.concatenate([w_pairs[0], bias_rows], 0), "batch", axis=1, tiled=True
    )
    weight_cols = weight_bias[:pair_count]
    bias_float = weight_bias[pair_count].astype(f32)

    received_wide = received.astype(f32)
    mine_wide = mine.astype(f32)
    product_all = (mine_wide * received_wide).astype(bf16)
    slot_index = jnp.arange(fields - 1, dtype=jnp.int32)[:, None, None]
    pair_rows = jnp.where(slot_index >= my_field, product_all[1:], product_all[:-1])
    pair_rows = pair_rows.reshape(pair_count, sample_rows)

    partial_hidden = lax.dot_general(
        pair_rows, weight_cols, (((0,), (0,)), ((), ())), preferred_element_type=f32
    )
    shares = lax.all_to_all(
        partial_hidden.astype(bf16).reshape(fields, own_rows, hidden_units),
        "field", split_axis=0, concat_axis=0, tiled=True,
    )
    preact = jnp.sum(shares.astype(f32), 0) + bias_float[None, :]
    gate_value = jax.nn.sigmoid(preact)
    own_grad = lax.dynamic_slice(grad_act, (my_field * own_rows, 0), (own_rows, hidden_units))
    own_slope = (
        own_grad.astype(f32) * gate_value * (1.0 + preact * (1.0 - gate_value))
    ).astype(bf16)
    slope_act = lax.all_to_all(
        jnp.broadcast_to(own_slope[None], (fields, own_rows, hidden_units)),
        "field", split_axis=0, concat_axis=0, tiled=True,
    ).reshape(sample_rows, hidden_units)

    pair_grad = lax.dot_general(
        weight_cols, slope_act, (((1,), (1,)), ((), ())), preferred_element_type=f32
    ).reshape(fields - 1, half_depth, sample_rows)
    zero_slot = jnp.zeros((1, half_depth, sample_rows), f32)
    below_slots = jnp.concatenate([pair_grad, zero_slot], 0)
    above_slots = jnp.concatenate([zero_slot, pair_grad], 0)
    dense_grad = jnp.where(
        partner < my_field, below_slots, jnp.where(partner > my_field, above_slots, 0.0)
    )
    returned = lax.all_to_all(
        (dense_grad * mine_wide).astype(bf16), "field", split_axis=0, concat_axis=0, tiled=True
    ).astype(f32)

    weight_term = lax.dot_general(
        pair_rows, slope_act, (((1,), (0,)), ((), ())), preferred_element_type=f32
    ).astype(bf16)
    unit_cols = hidden_units // shards
    weight_shares = lax.all_to_all(
        weight_term.reshape(pair_count, shards, unit_cols).transpose(1, 0, 2),
        "batch", split_axis=0, concat_axis=0, tiled=True,
    )
    weight_grad = jnp.sum(weight_shares.astype(f32), 0)

    local_part = dense_grad * received_wide
    full_grad = jnp.concatenate(
        [
            jnp.where(upper_half, returned, local_part),
            jnp.where(upper_half, local_part, returned),
        ],
        1,
    )
    full_grad = full_grad / jnp.sqrt(counts[:, 0].astype(f32))[None, None, :]
    entry_grad = full_grad.astype(bf16).reshape(fields * depth, sample_rows).T
    return entry_grad[:, None, :], weight_grad[None]


def solution(mesh):
    in_specs = (
        P("batch", "field", None),
        P("batch", "field"),
        P("field", None, "batch"),
        P("batch"),
        P("batch", None),
    )
    out_specs = (P("batch", "field", None), P("field", None, "batch"))
    return jax.shard_map(body, mesh=mesh, in_specs=in_specs, out_specs=out_specs, check_vma=False)
```

```python
import jax
import jax.numpy as jnp
from jax import lax
from jax.experimental import pallas as pl
from jax.experimental.pallas import tpu as pltpu
from jax.sharding import Mesh
from jax.sharding import PartitionSpec as P

f32, bf16 = jnp.float32, jnp.bfloat16
GROUP = 8


def upper_of(field_ref, block):
    partner = lax.broadcasted_iota(jnp.int32, (GROUP, 1, 1), 0) + block * GROUP
    return partner < field_ref[0]


def split_kernel(field_ref, pooled_ref, outbound_ref, mine_ref):
    half = outbound_ref.shape[1]
    turned = pooled_ref[...].astype(f32).T.reshape(GROUP, 2 * half, -1)
    low, high = turned[:, :half], turned[:, half:]
    upper = upper_of(field_ref, pl.program_id(0))
    outbound_ref[...] = jnp.where(upper, low, high).astype(bf16)
    mine_ref[...] = jnp.where(upper, high, low).astype(bf16)


def join_kernel(field_ref, root_ref, returned_ref, local_ref, entry_ref):
    returned = returned_ref[...].astype(f32) / root_ref[...][None]
    local = local_ref[...].astype(f32)
    upper = upper_of(field_ref, pl.program_id(0))
    low, high = jnp.where(upper, returned, local), jnp.where(upper, local, returned)
    turned = jnp.concatenate([low, high], 1)
    entry_ref[...] = turned.reshape(-1, turned.shape[2]).T.astype(bf16)


def pair_grad_kernel(root_ref, weight_ref, slope_ref, mine_ref, received_ref, out_ref, local_ref):
    pair_grad = lax.dot_general(
        weight_ref[...], slope_ref[...], (((1,), (1,)), ((), ())), preferred_element_type=f32
    )
    out_ref[...] = (pair_grad * mine_ref[...].astype(f32)).astype(bf16)
    local = pair_grad * received_ref[...].astype(f32)
    local_ref[...] = (local / root_ref[...]).astype(bf16)


def weight_kernel(core_ref, product_ref, slope_ref, sent_ref, kept_ref):
    term = jnp.dot(product_ref[...], slope_ref[...], preferred_element_type=f32)
    cols = term.shape[1] // 2
    first = core_ref[0] == 0
    sent_ref[0] = jnp.where(first, term[:, cols:], term[:, :cols]).astype(bf16)
    kept_ref[0] = jnp.where(first, term[:, :cols], term[:, cols:])


def body(pooled, counts, w_pairs, bias_terms, grad_act):
    sample_rows = pooled.shape[0]
    fields = lax.axis_size("field")
    depth = pooled.shape[2] // fields
    half = depth // 2
    hidden_units = grad_act.shape[1]
    pair_count = w_pairs.shape[1]
    own_rows = sample_rows // fields
    rows = fields * half
    my_field = lax.axis_index("field")
    field_scalar = my_field.astype(jnp.int32).reshape(1)
    smem = pl.BlockSpec(memory_space=pltpu.SMEM)
    root = jnp.sqrt(counts[:, 0].astype(f32))[None, :]

    half_block = pl.BlockSpec((GROUP, half, sample_rows), lambda i: (i, 0, 0))
    wide_block = pl.BlockSpec((sample_rows, GROUP * depth), lambda i: (0, i))
    half_shape = jax.ShapeDtypeStruct((fields, half, sample_rows), bf16)
    outbound, mine = pl.pallas_call(
        split_kernel,
        grid=(fields // GROUP,),
        in_specs=[smem, wide_block],
        out_specs=[half_block, half_block],
        out_shape=[half_shape, half_shape],
        name="split",
    )(field_scalar, pooled[:, 0])
    received = lax.all_to_all(outbound, "field", split_axis=0, concat_axis=0, tiled=True)

    weight_bias = lax.all_gather(
        jnp.concatenate([w_pairs[0], bias_terms[None, :]], 0), ("x", "core"), axis=1, tiled=True
    )
    bias_float = weight_bias[pair_count].astype(f32)
    row = jnp.arange(rows, dtype=jnp.int32)[:, None]
    low_rows = jnp.pad(weight_bias[:pair_count], ((0, half), (0, 0)))
    high_rows = jnp.pad(weight_bias[:pair_count], ((half, 0), (0, 0)))
    own_start = my_field * half
    weight_rows = jnp.where(
        row < own_start, low_rows, jnp.where(row >= own_start + half, high_rows, 0)
    )

    mine = mine.reshape(rows, sample_rows)
    received = received.reshape(rows, sample_rows)
    products = (mine.astype(f32) * received.astype(f32)).astype(bf16)
    partial_hidden = lax.dot_general(
        products, weight_rows, (((0,), (0,)), ((), ())), preferred_element_type=f32
    )
    shares = lax.all_to_all(
        partial_hidden.astype(bf16).reshape(fields, own_rows, hidden_units),
        "field", split_axis=0, concat_axis=0, tiled=True,
    )
    preact = jnp.sum(shares.astype(f32), 0) + bias_float[None, :]
    gate_value = jax.nn.sigmoid(preact)
    own_grad = lax.dynamic_slice(grad_act, (my_field * own_rows, 0), (own_rows, hidden_units))
    own_slope = (
        own_grad.astype(f32) * gate_value * (1.0 + preact * (1.0 - gate_value))
    ).astype(bf16)
    slope_act = lax.all_to_all(
        jnp.broadcast_to(own_slope[None], (fields, own_rows, hidden_units)),
        "field", split_axis=0, concat_axis=0, tiled=True,
    ).reshape(sample_rows, hidden_units)

    tall = 256
    row_block = pl.BlockSpec((tall, sample_rows), lambda i: (i, 0))
    row_shape = jax.ShapeDtypeStruct((rows, sample_rows), bf16)
    outgoing, local = pl.pallas_call(
        pair_grad_kernel,
        grid=(rows // tall,),
        in_specs=[
            pl.BlockSpec((1, sample_rows), lambda i: (0, 0)),
            pl.BlockSpec((tall, hidden_units), lambda i: (i, 0)),
            pl.BlockSpec((sample_rows, hidden_units), lambda i: (0, 0)),
            row_block,
            row_block,
        ],
        out_specs=[row_block, row_block],
        out_shape=[row_shape, row_shape],
        name="pairgrad",
    )(root, weight_rows, slope_act, mine, received)
    returned = lax.all_to_all(
        outgoing.reshape(fields, half, sample_rows),
        "field", split_axis=0, concat_axis=0, tiled=True,
    )

    cores, chips = lax.axis_size("core"), lax.axis_size("x")
    my_core, my_chip = lax.axis_index("core"), lax.axis_index("x")
    unit_cols = hidden_units // (cores * chips)
    term_block = pl.BlockSpec((1, rows, unit_cols), lambda i: (i, 0, 0))
    core_sent, core_kept = pl.pallas_call(
        weight_kernel,
        grid=(chips,),
        in_specs=[
            smem,
            pl.BlockSpec((rows, sample_rows), lambda i: (0, 0)),
            pl.BlockSpec((sample_rows, cores * unit_cols), lambda i: (0, i)),
        ],
        out_specs=[term_block, term_block],
        out_shape=[
            jax.ShapeDtypeStruct((chips, rows, unit_cols), bf16),
            jax.ShapeDtypeStruct((chips, rows, unit_cols), f32),
        ],
        name="weightterm",
    )(my_core.astype(jnp.int32).reshape(1), products, slope_act)
    core_got = lax.ppermute(core_sent, "core", [(0, 1), (1, 0)])
    chip_sum = core_kept + core_got.astype(f32)
    weight_total = lax.dynamic_index_in_dim(chip_sum, my_chip, 0, keepdims=False)
    for step in range(1, chips):
        chip_sent = lax.dynamic_index_in_dim(
            chip_sum, (my_chip + step) % chips, 0, keepdims=False
        ).astype(bf16)
        chip_got = lax.ppermute(
            chip_sent, "x", [(i, (i + step) % chips) for i in range(chips)]
        )
        weight_total = weight_total + chip_got.astype(f32)
    pair_row = jnp.arange(pair_count, dtype=jnp.int32)[:, None]
    weight_grad = jnp.where(pair_row >= own_start, weight_total[half:], weight_total[:-half])

    entry_grad = pl.pallas_call(
        join_kernel,
        grid=(fields // GROUP,),
        in_specs=[
            smem,
            pl.BlockSpec((1, sample_rows), lambda i: (0, 0)),
            half_block,
            half_block,
        ],
        out_specs=wide_block,
        out_shape=jax.ShapeDtypeStruct((sample_rows, fields * depth), bf16),
        name="join",
    )(field_scalar, root, returned, local.reshape(fields, half, sample_rows))
    return entry_grad[:, None, :], weight_grad[None]


def solution(mesh):
    fields = mesh.shape["field"]
    split = Mesh(
        mesh.devices.reshape(fields, mesh.shape["batch"] // 2, 2), ("field", "x", "core")
    )
    batch = ("x", "core")
    in_specs = (
        P(batch, "field", None),
        P(batch, "field"),
        P("field", None, batch),
        P(batch),
        P(batch, None),
    )
    out_specs = (P(batch, "field", None), P("field", None, batch))
    return jax.shard_map(body, mesh=split, in_specs=in_specs, out_specs=out_specs, check_vma=False)
```

```python
import jax
import jax.numpy as jnp
from jax import lax
from jax.experimental.layout import Layout, with_layout_constraint
from jax.sharding import Mesh
from jax.sharding import PartitionSpec as P

f32, bf16 = jnp.float32, jnp.bfloat16


def row_major(array):
    return with_layout_constraint(array, Layout(major_to_minor=tuple(range(array.ndim))))


def exchange(blocks):
    return lax.all_to_all(blocks, "field", split_axis=0, concat_axis=0, tiled=True)


def body(pooled, counts, w_pairs, bias_terms, grad_act):
    sample_rows = pooled.shape[0]
    fields = lax.axis_size("field")
    depth = pooled.shape[2] // fields
    half = depth // 2
    hidden_units = grad_act.shape[1]
    pair_count = w_pairs.shape[1]
    own_units = hidden_units // fields
    my_field = lax.axis_index("field")

    embedded = pooled.reshape(sample_rows, fields, depth).transpose(1, 2, 0)
    partner = jnp.arange(fields, dtype=jnp.int32)[:, None, None]
    upper = partner < my_field
    mine = jnp.where(upper, embedded[:, half:], embedded[:, :half])
    outbound = jnp.where(upper, embedded[:, :half], embedded[:, half:])
    received = exchange(outbound)
    weight_turned = row_major(
        lax.all_gather(row_major(w_pairs[0].T), ("x", "core"), axis=0, tiled=True)
    )

    received_wide, mine_wide = received.astype(f32), mine.astype(f32)
    products = (mine_wide * received_wide).astype(bf16)
    slot = jnp.arange(fields - 1, dtype=jnp.int32)[:, None, None]
    pair_rows = jnp.where(slot >= my_field, products[1:], products[:-1])
    pair_rows = pair_rows.reshape(pair_count, sample_rows)

    partial_hidden = jnp.dot(weight_turned, pair_rows, preferred_element_type=f32)
    partial_hidden = row_major(partial_hidden.astype(bf16))
    shares = exchange(partial_hidden.reshape(fields, own_units, sample_rows))

    bias_wide = lax.all_gather(bias_terms, ("x", "core"), axis=0, tiled=True)
    own_start = my_field * own_units
    own_bias = lax.dynamic_slice(bias_wide.reshape(-1, 1), (own_start, 0), (own_units, 1))
    own_grad = lax.dynamic_slice(grad_act, (0, own_start), (sample_rows, own_units)).T
    slot_row = (jnp.arange(fields * half, dtype=jnp.int32) // half)[:, None]
    weight_pairs = weight_turned.T
    below = jnp.pad(weight_pairs, ((0, half), (0, 0)))
    above = jnp.pad(weight_pairs, ((half, 0), (0, 0)))
    weight_rows = row_major(
        jnp.where(slot_row < my_field, below, jnp.where(slot_row > my_field, above, 0))
    )

    preact = jnp.sum(shares.astype(f32), 0) + own_bias.astype(f32)
    gate_value = jax.nn.sigmoid(preact)
    own_slope = (
        own_grad.astype(f32) * gate_value * (1.0 + preact * (1.0 - gate_value))
    ).astype(bf16)
    slope_turned = exchange(
        jnp.broadcast_to(own_slope[None], (fields, own_units, sample_rows))
    ).reshape(hidden_units, sample_rows)

    pair_grad = jnp.dot(weight_rows, slope_turned, preferred_element_type=f32)
    pair_grad = pair_grad.reshape(fields, half, sample_rows)
    outgoing = (pair_grad * mine_wide).astype(bf16)
    returned = exchange(outgoing).astype(f32)

    cores, chips = lax.axis_size("core"), lax.axis_size("x")
    my_core, my_chip = lax.axis_index("core"), lax.axis_index("x")
    term = lax.dot_general(
        slope_turned, pair_rows, (((1,), (1,)), ((), ())), preferred_element_type=f32
    )
    term = term.reshape(chips, cores, hidden_units // (chips * cores), pair_count)
    core_sent = lax.dynamic_index_in_dim(term, 1 - my_core, 1, keepdims=False).astype(bf16)
    core_kept = lax.dynamic_index_in_dim(term, my_core, 1, keepdims=False)
    core_got = lax.ppermute(core_sent, "core", [(0, 1), (1, 0)])
    chip_sum = core_kept + core_got.astype(f32)
    weight_total = lax.dynamic_index_in_dim(chip_sum, my_chip, 0, keepdims=False)
    for step in range(1, chips):
        chip_sent = lax.dynamic_index_in_dim(
            chip_sum, (my_chip + step) % chips, 0, keepdims=False
        ).astype(bf16)
        chip_got = lax.ppermute(
            chip_sent, "x", [(i, (i + step) % chips) for i in range(chips)]
        )
        weight_total = weight_total + chip_got.astype(f32)

    local = pair_grad * received_wide
    full = jnp.concatenate(
        [jnp.where(upper, returned, local), jnp.where(upper, local, returned)], 1
    )
    full = full / jnp.sqrt(counts[:, 0].astype(f32))[None, None, :]
    turned = row_major(full.astype(bf16).reshape(fields * depth, sample_rows))
    return turned.T[:, None, :], weight_total.T[None]


def solution(mesh):
    fields = mesh.shape["field"]
    split = Mesh(
        mesh.devices.reshape(fields, mesh.shape["batch"] // 2, 2), ("field", "x", "core")
    )
    batch = ("x", "core")
    in_specs = (
        P(batch, "field", None),
        P(batch, "field"),
        P("field", None, batch),
        P(batch),
        P(batch, None),
    )
    out_specs = (P(batch, "field", None), P("field", None, batch))
    return jax.shard_map(body, mesh=split, in_specs=in_specs, out_specs=out_specs, check_vma=False)
```

```python
import jax
import jax.numpy as jnp
from jax import lax
from jax.experimental.layout import Layout, with_layout_constraint
from jax.experimental import pallas as pl
from jax.experimental.pallas import tpu as pltpu
from jax.sharding import Mesh
from jax.sharding import PartitionSpec as P

f32, bf16 = jnp.float32, jnp.bfloat16


def row_major(array):
    return with_layout_constraint(array, Layout(major_to_minor=tuple(range(array.ndim))))


def exchange(blocks):
    return lax.all_to_all(blocks, "field", split_axis=0, concat_axis=0, tiled=True)


def grad_kernel(place_ref, grad_ref, own_ref, turned_ref):
    turned_ref[...] = grad_ref[...].astype(f32).T
    rows = own_ref.shape[0]
    own_ref[...] = turned_ref[pl.ds(pl.multiple_of(place_ref[1] * rows, rows), rows), :]


def own_columns(grad_act, shard, place, units, shard_units):
    samples = grad_act.shape[0]
    return pl.pallas_call(
        grad_kernel,
        grid_spec=pltpu.PrefetchScalarGridSpec(
            num_scalar_prefetch=1,
            grid=(1,),
            in_specs=[pl.BlockSpec((samples, shard_units), lambda i, place: (0, place[0]))],
            out_specs=pl.BlockSpec((units, samples), lambda i, place: (0, 0)),
            scratch_shapes=[pltpu.VMEM((shard_units, samples), f32)],
        ),
        out_shape=jax.ShapeDtypeStruct((units, samples), f32),
        name="owngrad",
    )(jnp.stack([shard, place]).astype(jnp.int32), grad_act)


def body(pooled, counts, w_pairs, bias_terms, grad_act):
    sample_rows = pooled.shape[0]
    fields = lax.axis_size("field")
    depth = pooled.shape[2] // fields
    half = depth // 2
    hidden_units = grad_act.shape[1]
    pair_count = w_pairs.shape[1]
    own_units = hidden_units // fields
    my_field = lax.axis_index("field")

    embedded = pooled.reshape(sample_rows, fields, depth).transpose(1, 2, 0)
    partner = jnp.arange(fields, dtype=jnp.int32)[:, None, None]
    upper = partner < my_field
    mine = jnp.where(upper, embedded[:, half:], embedded[:, :half])
    outbound = jnp.where(upper, embedded[:, :half], embedded[:, half:])
    received = exchange(outbound)
    chip_weights = lax.all_gather(row_major(w_pairs[0].T), "x", axis=0, tiled=True)
    weight_turned = row_major(
        lax.all_gather(row_major(chip_weights), "core", axis=0, tiled=True)
    )

    received_wide, mine_wide = received.astype(f32), mine.astype(f32)
    products = (mine_wide * received_wide).astype(bf16)
    slot = jnp.arange(fields - 1, dtype=jnp.int32)[:, None, None]
    pair_rows = jnp.where(slot >= my_field, products[1:], products[:-1])
    pair_rows = pair_rows.reshape(pair_count, sample_rows)

    partial_hidden = jnp.dot(weight_turned, pair_rows, preferred_element_type=f32)
    partial_hidden = row_major(partial_hidden.astype(bf16))
    shares = exchange(partial_hidden.reshape(fields, own_units, sample_rows))
    other_rows = lax.ppermute(pair_rows, "core", [(0, 1), (1, 0)])

    bias_wide = lax.all_gather(bias_terms, ("x", "core"), axis=0, tiled=True)
    cores, chips = lax.axis_size("core"), lax.axis_size("x")
    my_core, my_chip = lax.axis_index("core"), lax.axis_index("x")
    shard_units = hidden_units // (cores * chips)
    own_place = my_field * own_units
    own_shard = own_place // shard_units
    own_shard = (own_shard % chips) * cores + own_shard // chips
    own_start = own_shard * shard_units + own_place % shard_units
    own_bias = lax.dynamic_slice(bias_wide.reshape(-1, 1), (own_start, 0), (own_units, 1))
    own_grad = own_columns(
        grad_act, own_shard, own_place % shard_units // own_units, own_units, shard_units
    )
    slot_row = (jnp.arange(fields * half, dtype=jnp.int32) // half)[:, None]
    weight_pairs = weight_turned.T
    below = jnp.pad(weight_pairs, ((0, half), (0, 0)))
    above = jnp.pad(weight_pairs, ((half, 0), (0, 0)))
    weight_rows = lax.optimization_barrier(
        row_major(
            jnp.where(slot_row < my_field, below, jnp.where(slot_row > my_field, above, 0))
        )
    )

    preact = jnp.sum(shares.astype(f32), 0) + own_bias.astype(f32)
    gate_value = jax.nn.sigmoid(preact)
    own_slope = (
        own_grad * gate_value * (1.0 + preact * (1.0 - gate_value))
    ).astype(bf16)
    slope_turned = exchange(
        jnp.broadcast_to(own_slope[None], (fields, own_units, sample_rows))
    ).reshape(hidden_units, sample_rows)

    pair_grad = lax.optimization_barrier(
        jnp.dot(weight_rows, slope_turned, preferred_element_type=f32)
    )
    pair_grad = pair_grad.reshape(fields, half, sample_rows)
    outgoing = (pair_grad * mine_wide).astype(bf16)
    returned = exchange(outgoing).astype(f32)

    halves = slope_turned.reshape(cores, chips, shard_units, sample_rows)
    kept = lax.dynamic_index_in_dim(halves, my_core, 0, keepdims=False)
    sent = lax.dynamic_index_in_dim(halves, 1 - my_core, 0, keepdims=False)
    got = lax.ppermute(sent, "core", [(0, 1), (1, 0)])
    chip_sum = lax.dot_general(
        kept, pair_rows, (((2,), (1,)), ((), ())), preferred_element_type=f32
    )
    chip_sum = chip_sum + lax.dot_general(
        got, other_rows, (((2,), (1,)), ((), ())), preferred_element_type=f32
    )
    weight_total = lax.dynamic_index_in_dim(chip_sum, my_chip, 0, keepdims=False)
    for step in range(1, chips):
        chip_sent = lax.dynamic_index_in_dim(
            chip_sum, (my_chip + step) % chips, 0, keepdims=False
        ).astype(bf16)
        chip_got = lax.ppermute(
            chip_sent, "x", [(i, (i + step) % chips) for i in range(chips)]
        )
        weight_total = weight_total + chip_got.astype(f32)

    local = pair_grad * received_wide
    full = jnp.concatenate(
        [jnp.where(upper, returned, local), jnp.where(upper, local, returned)], 1
    )
    full = full / jnp.sqrt(counts[:, 0].astype(f32))[None, None, :]
    turned = row_major(full.astype(bf16).reshape(fields * depth, sample_rows))
    entry_grad = turned.T[:, None, :]
    return entry_grad, weight_total.T[None]


def solution(mesh):
    fields = mesh.shape["field"]
    split = Mesh(
        mesh.devices.reshape(fields, mesh.shape["batch"] // 2, 2), ("field", "x", "core")
    )
    batch = ("x", "core")
    in_specs = (
        P(batch, "field", None),
        P(batch, "field"),
        P("field", None, batch),
        P(batch),
        P(batch, None),
    )
    out_specs = (P(batch, "field", None), P("field", None, batch))
    return jax.shard_map(body, mesh=split, in_specs=in_specs, out_specs=out_specs, check_vma=False)
```

```python
import jax
import jax.numpy as jnp
from jax import lax
from jax.experimental.layout import Layout, with_layout_constraint
from jax.experimental import pallas as pl
from jax.experimental.pallas import tpu as pltpu
from jax.sharding import Mesh
from jax.sharding import PartitionSpec as P

f32, bf16 = jnp.float32, jnp.bfloat16


def row_major(array):
    return with_layout_constraint(array, Layout(major_to_minor=tuple(range(array.ndim))))


def exchange(blocks):
    return lax.all_to_all(blocks, "field", split_axis=0, concat_axis=0, tiled=True)


def grad_kernel(place_ref, grad_ref, own_ref, turned_ref):
    turned_ref[...] = grad_ref[...].astype(f32).T
    rows = own_ref.shape[0]
    own_ref[...] = turned_ref[pl.ds(pl.multiple_of(place_ref[1] * rows, rows), rows), :]


def own_columns(grad_act, shard, place, units, shard_units):
    samples = grad_act.shape[0]
    return pl.pallas_call(
        grad_kernel,
        grid_spec=pltpu.PrefetchScalarGridSpec(
            num_scalar_prefetch=1,
            grid=(1,),
            in_specs=[pl.BlockSpec((samples, shard_units), lambda i, place: (0, place[0]))],
            out_specs=pl.BlockSpec((units, samples), lambda i, place: (0, 0)),
            scratch_shapes=[pltpu.VMEM((shard_units, samples), f32)],
        ),
        out_shape=jax.ShapeDtypeStruct((units, samples), f32),
        name="owngrad",
    )(jnp.stack([shard, place]).astype(jnp.int32), grad_act)


def body(pooled, counts, w_pairs, bias_terms, grad_act):
    sample_rows = pooled.shape[0]
    fields = lax.axis_size("field")
    depth = pooled.shape[2] // fields
    half = depth // 2
    hidden_units = grad_act.shape[1]
    pair_count = w_pairs.shape[1]
    own_units = hidden_units // fields
    my_field = lax.axis_index("field")

    embedded = pooled.reshape(sample_rows, fields, depth).transpose(1, 2, 0)
    partner = jnp.arange(fields, dtype=jnp.int32)[:, None, None]
    upper = partner < my_field
    mine = jnp.where(upper, embedded[:, half:], embedded[:, :half])
    outbound = jnp.where(upper, embedded[:, :half], embedded[:, half:])
    received = exchange(outbound)
    chip_weights = lax.all_gather(row_major(w_pairs[0].T), "x", axis=0, tiled=True)
    weight_turned = row_major(
        lax.all_gather(row_major(chip_weights), "core", axis=0, tiled=True)
    )

    received_wide, mine_wide = received.astype(f32), mine.astype(f32)
    products = (mine_wide * received_wide).astype(bf16)
    slot = jnp.arange(fields - 1, dtype=jnp.int32)[:, None, None]
    pair_rows = jnp.where(slot >= my_field, products[1:], products[:-1])
    pair_rows = pair_rows.reshape(pair_count, sample_rows)

    partial_hidden = jnp.dot(weight_turned, pair_rows, preferred_element_type=f32)
    partial_hidden = row_major(partial_hidden.astype(bf16))
    shares = exchange(partial_hidden.reshape(fields, own_units, sample_rows))
    other_rows = lax.ppermute(pair_rows, "core", [(0, 1), (1, 0)])

    bias_wide = lax.all_gather(bias_terms, ("x", "core"), axis=0, tiled=True)
    cores, chips = lax.axis_size("core"), lax.axis_size("x")
    my_core, my_chip = lax.axis_index("core"), lax.axis_index("x")
    shard_units = hidden_units // (cores * chips)
    own_place = my_field * own_units
    own_shard = own_place // shard_units
    own_shard = (own_shard % chips) * cores + own_shard // chips
    own_start = own_shard * shard_units + own_place % shard_units
    own_bias = lax.dynamic_slice(bias_wide.reshape(-1, 1), (own_start, 0), (own_units, 1))
    own_grad = own_columns(
        grad_act, own_shard, own_place % shard_units // own_units, own_units, shard_units
    )
    slot_row = (jnp.arange(fields * half, dtype=jnp.int32) // half)[:, None]
    weight_pairs = weight_turned.T
    below = jnp.pad(weight_pairs, ((0, half), (0, 0)))
    above = jnp.pad(weight_pairs, ((half, 0), (0, 0)))
    weight_rows = lax.optimization_barrier(
        row_major(
            jnp.where(slot_row < my_field, below, jnp.where(slot_row > my_field, above, 0))
        )
    )

    preact = jnp.sum(shares.astype(f32), 0) + own_bias.astype(f32)
    gate_value = jax.nn.sigmoid(preact)
    own_slope = (
        own_grad * gate_value * (1.0 + preact * (1.0 - gate_value))
    ).astype(bf16)
    slope_turned = exchange(
        jnp.broadcast_to(own_slope[None], (fields, own_units, sample_rows))
    ).reshape(hidden_units, sample_rows)

    pair_grad = lax.optimization_barrier(
        jnp.dot(weight_rows, slope_turned, preferred_element_type=f32)
    )
    pair_grad = pair_grad.reshape(fields, half, sample_rows)
    outgoing = (pair_grad * mine_wide).astype(bf16)
    returned = exchange(outgoing).astype(f32)

    halves = slope_turned.reshape(cores, chips, shard_units, sample_rows)
    kept = lax.dynamic_index_in_dim(halves, my_core, 0, keepdims=False)
    sent = lax.dynamic_index_in_dim(halves, 1 - my_core, 0, keepdims=False)
    got = lax.ppermute(sent, "core", [(0, 1), (1, 0)])
    chip_sum = lax.dot_general(
        kept, pair_rows, (((2,), (1,)), ((), ())), preferred_element_type=f32
    )
    chip_sum = chip_sum + lax.dot_general(
        got, other_rows, (((2,), (1,)), ((), ())), preferred_element_type=f32
    )
    blocks = [
        lax.dynamic_index_in_dim(chip_sum, (my_chip + step) % chips, 0, keepdims=False)
        for step in range(chips)
    ]
    weight_total, *blocks = lax.optimization_barrier(
        (blocks[0], *[block.astype(bf16) for block in blocks[1:]])
    )
    for step, block in enumerate(blocks, 1):
        chip_got = lax.ppermute(
            block, "x", [(i, (i + step) % chips) for i in range(chips)]
        )
        weight_total = weight_total + chip_got.astype(f32)

    local = pair_grad * received_wide
    full = jnp.concatenate(
        [jnp.where(upper, returned, local), jnp.where(upper, local, returned)], 1
    )
    full = full / jnp.sqrt(counts[:, 0].astype(f32))[None, None, :]
    turned = row_major(full.astype(bf16).reshape(fields * depth, sample_rows))
    entry_grad = turned.T[:, None, :]
    return entry_grad, weight_total.T[None]


def solution(mesh):
    fields = mesh.shape["field"]
    split = Mesh(
        mesh.devices.reshape(fields, mesh.shape["batch"] // 2, 2), ("field", "x", "core")
    )
    batch = ("x", "core")
    in_specs = (
        P(batch, "field", None),
        P(batch, "field"),
        P("field", None, batch),
        P(batch),
        P(batch, None),
    )
    out_specs = (P(batch, "field", None), P("field", None, batch))
    return jax.shard_map(body, mesh=split, in_specs=in_specs, out_specs=out_specs, check_vma=False)
```

```python
import jax
import jax.numpy as jnp
from jax import lax
from jax.experimental.layout import Layout, with_layout_constraint
from jax.experimental import pallas as pl
from jax.experimental.pallas import tpu as pltpu
from jax.sharding import Mesh
from jax.sharding import PartitionSpec as P

f32, bf16 = jnp.float32, jnp.bfloat16


def row_major(array):
    return with_layout_constraint(array, Layout(major_to_minor=tuple(range(array.ndim))))


FIELD = ("z1", "z0", "y1", "y0")
NEAR, FAR = ("z0", "y0"), ("z1", "y1")


def exchange(blocks, axes=FIELD):
    return lax.all_to_all(blocks, axes, split_axis=0, concat_axis=0, tiled=True)


def grad_kernel(place_ref, grad_ref, own_ref, turned_ref):
    turned_ref[...] = grad_ref[...].astype(f32).T
    rows = own_ref.shape[0]
    start = pl.multiple_of(place_ref[1] * rows, rows)
    own_ref[...] = turned_ref[pl.ds(start, rows), :].astype(bf16)


def own_columns(grad_act, shard, place, units, shard_units):
    samples = grad_act.shape[0]
    return pl.pallas_call(
        grad_kernel,
        grid_spec=pltpu.PrefetchScalarGridSpec(
            num_scalar_prefetch=1,
            grid=(1,),
            in_specs=[pl.BlockSpec((samples, shard_units), lambda i, place: (0, place[0]))],
            out_specs=pl.BlockSpec((units, samples), lambda i, place: (0, 0)),
            scratch_shapes=[pltpu.VMEM((shard_units, samples), f32)],
        ),
        out_shape=jax.ShapeDtypeStruct((units, samples), bf16),
        name="owngrad",
    )(jnp.stack([shard, place]).astype(jnp.int32), grad_act)


def body(pooled, counts, w_pairs, bias_terms, grad_act):
    sample_rows = pooled.shape[0]
    fields = lax.axis_size(FIELD)
    depth = pooled.shape[2] // fields
    half = depth // 2
    hidden_units = grad_act.shape[1]
    pair_count = w_pairs.shape[1]
    own_units = hidden_units // fields
    my_field = lax.axis_index(FIELD)

    embedded = pooled.reshape(sample_rows, fields, depth).transpose(1, 2, 0)
    partner = jnp.arange(fields, dtype=jnp.int32)[:, None, None]
    upper = partner < my_field
    mine = jnp.where(upper, embedded[:, half:], embedded[:, :half])
    outbound = jnp.where(upper, embedded[:, :half], embedded[:, half:])
    received = exchange(outbound)
    shard = jnp.concatenate([w_pairs[0], bias_terms[None, :]], 0).T
    weight_turned = row_major(
        lax.all_gather(row_major(shard), ("x", "core"), axis=0, tiled=True)
    )

    received_wide, mine_wide = received.astype(f32), mine.astype(f32)
    products = (mine_wide * received_wide).astype(bf16)
    slot = jnp.arange(fields - 1, dtype=jnp.int32)[:, None, None]
    pair_rows = jnp.where(slot >= my_field, products[1:], products[:-1])
    pair_rows = pair_rows.reshape(pair_count, sample_rows)

    biased_rows = jnp.concatenate([pair_rows, jnp.zeros((1, sample_rows), bf16)], 0)
    partial_hidden = jnp.dot(weight_turned, biased_rows, preferred_element_type=f32)
    partial_hidden = row_major(partial_hidden.astype(bf16))
    near, far = lax.axis_size(NEAR), lax.axis_size(FAR)
    near_shares = exchange(partial_hidden.reshape(near, -1, sample_rows), NEAR)
    near_sum = jnp.sum(near_shares.astype(f32), 0).astype(bf16)
    shares = exchange(near_sum.reshape(far, own_units, sample_rows), FAR)
    other_rows = lax.ppermute(pair_rows, "core", [(0, 1), (1, 0)])

    cores, chips = lax.axis_size("core"), lax.axis_size("x")
    my_core, my_chip = lax.axis_index("core"), lax.axis_index("x")
    shard_units = hidden_units // (cores * chips)
    own_start = (lax.axis_index(NEAR) * far + lax.axis_index(FAR)) * own_units
    own_bias = lax.dynamic_slice(weight_turned, (own_start, pair_count), (own_units, 1))
    own_bias = lax.optimization_barrier(own_bias.astype(f32))
    own_grad = own_columns(
        grad_act,
        own_start // shard_units,
        own_start % shard_units // own_units,
        own_units,
        shard_units,
    )
    own_grad = lax.optimization_barrier(own_grad.astype(f32))
    slot_row = (jnp.arange(fields * half, dtype=jnp.int32) // half)[:, None]
    weight_pairs = weight_turned[:, :pair_count].T
    below = jnp.pad(weight_pairs, ((0, half), (0, 0)))
    above = jnp.pad(weight_pairs, ((half, 0), (0, 0)))
    weight_rows = lax.optimization_barrier(
        row_major(
            jnp.where(slot_row < my_field, below, jnp.where(slot_row > my_field, above, 0))
        )
    )

    preact = jnp.sum(shares.astype(f32), 0) + own_bias
    gate_value = jax.nn.sigmoid(preact)
    own_slope = (
        own_grad * gate_value * (1.0 + preact * (1.0 - gate_value))
    ).astype(bf16)
    far_slope = exchange(
        jnp.broadcast_to(own_slope[None], (far, own_units, sample_rows)), FAR
    ).reshape(1, far * own_units, sample_rows)
    slope_turned = exchange(
        jnp.broadcast_to(far_slope, (near, far * own_units, sample_rows)), NEAR
    ).reshape(hidden_units, sample_rows)

    pair_grad = lax.optimization_barrier(
        jnp.dot(weight_rows, slope_turned, preferred_element_type=f32)
    )
    pair_grad = pair_grad.reshape(fields, half, sample_rows)
    outgoing = (pair_grad * mine_wide).astype(bf16)
    returned = exchange(outgoing).astype(f32)

    halves = slope_turned.reshape(chips, cores, shard_units, sample_rows)
    kept = lax.dynamic_index_in_dim(halves, my_core, 1, keepdims=False)
    sent = lax.dynamic_index_in_dim(halves, 1 - my_core, 1, keepdims=False)
    got = lax.ppermute(sent, "core", [(0, 1), (1, 0)])
    chip_sum = lax.dot_general(
        kept, pair_rows, (((2,), (1,)), ((), ())), preferred_element_type=f32
    )
    chip_sum = chip_sum + lax.dot_general(
        got, other_rows, (((2,), (1,)), ((), ())), preferred_element_type=f32
    )
    blocks = [
        lax.dynamic_index_in_dim(chip_sum, (my_chip + step) % chips, 0, keepdims=False)
        for step in range(chips)
    ]
    weight_total, *blocks = lax.optimization_barrier(
        (blocks[0], *[block.astype(bf16) for block in blocks[1:]])
    )
    for step, block in enumerate(blocks, 1):
        chip_got = lax.ppermute(
            block, "x", [(i, (i + step) % chips) for i in range(chips)]
        )
        weight_total = weight_total + chip_got.astype(f32)

    local = pair_grad * received_wide
    full = jnp.concatenate(
        [jnp.where(upper, returned, local), jnp.where(upper, local, returned)], 1
    )
    full = full / jnp.sqrt(counts[:, 0].astype(f32))[None, None, :]
    turned = row_major(full.astype(bf16).reshape(fields * depth, sample_rows))
    entry_grad = turned.T[:, None, :]
    return entry_grad, weight_total.T[None]


def solution(mesh):
    split = Mesh(
        mesh.devices.reshape(4, 2, 4, 2, mesh.shape["batch"] // 2, 2), (*FIELD, "x", "core")
    )
    batch = ("x", "core")
    in_specs = (
        P(batch, FIELD, None),
        P(batch, FIELD),
        P(FIELD, None, batch),
        P(batch),
        P(batch, None),
    )
    out_specs = (P(batch, FIELD, None), P(FIELD, None, batch))
    return jax.shard_map(body, mesh=split, in_specs=in_specs, out_specs=out_specs, check_vma=False)
```

```python
import jax
import jax.numpy as jnp
from jax import lax
from jax.experimental.layout import Layout, with_layout_constraint
from jax.experimental import pallas as pl
from jax.experimental.pallas import tpu as pltpu
from jax.sharding import Mesh
from jax.sharding import PartitionSpec as P

f32, bf16 = jnp.float32, jnp.bfloat16


def row_major(array):
    return with_layout_constraint(array, Layout(major_to_minor=tuple(range(array.ndim))))


def exchange(blocks):
    return lax.all_to_all(blocks, "field", split_axis=0, concat_axis=0, tiled=True)


def grad_kernel(place_ref, grad_ref, own_ref, turned_ref):
    turned_ref[...] = grad_ref[...].astype(f32).T
    rows = own_ref.shape[0]
    start = pl.multiple_of(place_ref[1] * rows, rows)
    own_ref[...] = turned_ref[pl.ds(start, rows), :].astype(bf16)


def own_columns(grad_act, shard, place, units, shard_units):
    samples = grad_act.shape[0]
    return pl.pallas_call(
        grad_kernel,
        grid_spec=pltpu.PrefetchScalarGridSpec(
            num_scalar_prefetch=1,
            grid=(1,),
            in_specs=[pl.BlockSpec((samples, shard_units), lambda i, place: (0, place[0]))],
            out_specs=pl.BlockSpec((units, samples), lambda i, place: (0, 0)),
            scratch_shapes=[pltpu.VMEM((shard_units, samples), f32)],
        ),
        out_shape=jax.ShapeDtypeStruct((units, samples), bf16),
        name="owngrad",
    )(jnp.stack([shard, place]).astype(jnp.int32), grad_act)


def body(pooled, counts, w_pairs, bias_terms, grad_act):
    sample_rows = pooled.shape[0]
    fields = lax.axis_size("field")
    depth = pooled.shape[2] // fields
    half = depth // 2
    hidden_units = grad_act.shape[1]
    pair_count = w_pairs.shape[1]
    own_units = hidden_units // fields
    my_field = lax.axis_index("field")

    embedded = pooled.reshape(sample_rows, fields, depth).transpose(1, 2, 0)
    partner = jnp.arange(fields, dtype=jnp.int32)[:, None, None]
    upper = partner < my_field
    mine = jnp.where(upper, embedded[:, half:], embedded[:, :half])
    outbound = jnp.where(upper, embedded[:, :half], embedded[:, half:])
    received = exchange(outbound)
    weight_turned = row_major(
        lax.all_gather(row_major(w_pairs[0].T), ("x", "core"), axis=0, tiled=True)
    )

    received_wide, mine_wide = received.astype(f32), mine.astype(f32)
    products = (mine_wide * received_wide).astype(bf16)
    slot = jnp.arange(fields - 1, dtype=jnp.int32)[:, None, None]
    pair_rows = jnp.where(slot >= my_field, products[1:], products[:-1])
    pair_rows = pair_rows.reshape(pair_count, sample_rows)

    partial_hidden = jnp.dot(weight_turned, pair_rows, preferred_element_type=f32)
    partial_hidden = row_major(partial_hidden.astype(bf16))
    shares = exchange(partial_hidden.reshape(fields, own_units, sample_rows))
    other_rows = lax.ppermute(pair_rows, "core", [(0, 1), (1, 0)])

    bias_wide = lax.all_gather(bias_terms, ("x", "core"), axis=0, tiled=True)
    cores, chips = lax.axis_size("core"), lax.axis_size("x")
    my_core, my_chip = lax.axis_index("core"), lax.axis_index("x")
    shard_units = hidden_units // (cores * chips)
    own_start = my_field * own_units
    own_bias = lax.dynamic_slice(bias_wide.reshape(-1, 1), (own_start, 0), (own_units, 1))
    own_grad = own_columns(
        grad_act,
        own_start // shard_units,
        own_start % shard_units // own_units,
        own_units,
        shard_units,
    )
    own_grad = lax.optimization_barrier(own_grad.astype(f32))
    slot_row = (jnp.arange(fields * half, dtype=jnp.int32) // half)[:, None]
    weight_pairs = weight_turned.T
    below = jnp.pad(weight_pairs, ((0, half), (0, 0)))
    above = jnp.pad(weight_pairs, ((half, 0), (0, 0)))
    weight_rows = lax.optimization_barrier(
        row_major(
            jnp.where(slot_row < my_field, below, jnp.where(slot_row > my_field, above, 0))
        )
    )

    preact = jnp.sum(shares.astype(f32), 0) + own_bias.astype(f32)
    gate_value = jax.nn.sigmoid(preact)
    own_slope = (
        own_grad * gate_value * (1.0 + preact * (1.0 - gate_value))
    ).astype(bf16)
    slope_turned = exchange(
        jnp.broadcast_to(own_slope[None], (fields, own_units, sample_rows))
    ).reshape(hidden_units, sample_rows)

    pair_grad = lax.optimization_barrier(
        jnp.dot(weight_rows, slope_turned, preferred_element_type=f32)
    )
    pair_grad = pair_grad.reshape(fields, half, sample_rows)
    outgoing = (pair_grad * mine_wide).astype(bf16)
    returned = exchange(outgoing).astype(f32)

    halves = slope_turned.reshape(chips, cores, shard_units, sample_rows)
    kept = lax.dynamic_index_in_dim(halves, my_core, 1, keepdims=False)
    sent = lax.dynamic_index_in_dim(halves, 1 - my_core, 1, keepdims=False)
    got = lax.ppermute(sent, "core", [(0, 1), (1, 0)])
    chip_sum = lax.dot_general(
        kept, pair_rows, (((2,), (1,)), ((), ())), preferred_element_type=f32
    )
    chip_sum = chip_sum + lax.dot_general(
        got, other_rows, (((2,), (1,)), ((), ())), preferred_element_type=f32
    )
    blocks = [
        lax.dynamic_index_in_dim(chip_sum, (my_chip + step) % chips, 0, keepdims=False)
        for step in range(chips)
    ]
    weight_total, *blocks = lax.optimization_barrier(
        (blocks[0], *[block.astype(bf16) for block in blocks[1:]])
    )
    for step, block in enumerate(blocks, 1):
        chip_got = lax.ppermute(
            block, "x", [(i, (i + step) % chips) for i in range(chips)]
        )
        weight_total = weight_total + chip_got.astype(f32)

    local = pair_grad * received_wide
    full = jnp.concatenate(
        [jnp.where(upper, returned, local), jnp.where(upper, local, returned)], 1
    )
    full = full / jnp.sqrt(counts[:, 0].astype(f32))[None, None, :]
    turned = row_major(full.astype(bf16).reshape(fields * depth, sample_rows))
    entry_grad = turned.T[:, None, :]
    return entry_grad, weight_total.T[None]


def solution(mesh):
    fields = mesh.shape["field"]
    split = Mesh(
        mesh.devices.reshape(fields, mesh.shape["batch"] // 2, 2), ("field", "x", "core")
    )
    batch = ("x", "core")
    in_specs = (
        P(batch, "field", None),
        P(batch, "field"),
        P("field", None, batch),
        P(batch),
        P(batch, None),
    )
    out_specs = (P(batch, "field", None), P("field", None, batch))
    return jax.shard_map(body, mesh=split, in_specs=in_specs, out_specs=out_specs, check_vma=False)
```

```python
import jax
import jax.numpy as jnp
from jax import lax
from jax.experimental.layout import Layout, with_layout_constraint
from jax.experimental import pallas as pl
from jax.experimental.pallas import tpu as pltpu
from jax.sharding import Mesh
from jax.sharding import PartitionSpec as P

f32, bf16 = jnp.float32, jnp.bfloat16


def row_major(array):
    return with_layout_constraint(array, Layout(major_to_minor=tuple(range(array.ndim))))


def exchange(blocks):
    return lax.all_to_all(blocks, "field", split_axis=0, concat_axis=0, tiled=True)


def grad_kernel(place_ref, grad_ref, own_ref, turned_ref):
    turned_ref[...] = grad_ref[...].astype(f32).T
    rows = own_ref.shape[0]
    start = pl.multiple_of(place_ref[1] * rows, rows)
    own_ref[...] = turned_ref[pl.ds(start, rows), :].astype(bf16)


def own_columns(grad_act, shard, place, units, shard_units):
    samples = grad_act.shape[0]
    return pl.pallas_call(
        grad_kernel,
        grid_spec=pltpu.PrefetchScalarGridSpec(
            num_scalar_prefetch=1,
            grid=(1,),
            in_specs=[pl.BlockSpec((samples, shard_units), lambda i, place: (0, place[0]))],
            out_specs=pl.BlockSpec((units, samples), lambda i, place: (0, 0)),
            scratch_shapes=[pltpu.VMEM((shard_units, samples), f32)],
        ),
        out_shape=jax.ShapeDtypeStruct((units, samples), bf16),
        name="owngrad",
    )(jnp.stack([shard, place]).astype(jnp.int32), grad_act)


def body(pooled, counts, w_pairs, bias_terms, grad_act):
    sample_rows = pooled.shape[0]
    fields = lax.axis_size("field")
    depth = pooled.shape[2] // fields
    half = depth // 2
    hidden_units = grad_act.shape[1]
    pair_count = w_pairs.shape[1]
    own_units = hidden_units // fields
    my_field = lax.axis_index("field")

    embedded = pooled.reshape(sample_rows, fields, depth).transpose(1, 2, 0)
    partner = jnp.arange(fields, dtype=jnp.int32)[:, None, None]
    upper = partner < my_field
    mine = jnp.where(upper, embedded[:, half:], embedded[:, :half])
    outbound = jnp.where(upper, embedded[:, :half], embedded[:, half:])
    received = exchange(outbound)
    weight_turned = row_major(
        lax.all_gather(row_major(w_pairs[0].T), ("x", "core"), axis=0, tiled=True)
    )

    received_wide, mine_wide = received.astype(f32), mine.astype(f32)
    products = (mine_wide * received_wide).astype(bf16)
    slot = jnp.arange(fields - 1, dtype=jnp.int32)[:, None, None]
    pair_rows = jnp.where(slot >= my_field, products[1:], products[:-1])
    pair_rows = pair_rows.reshape(pair_count, sample_rows)

    partial_hidden = jnp.dot(weight_turned, pair_rows, preferred_element_type=f32)
    partial_hidden = row_major(partial_hidden.astype(bf16))
    shares = exchange(partial_hidden.reshape(fields, own_units, sample_rows))
    other_rows = lax.ppermute(pair_rows, "core", [(0, 1), (1, 0)])

    bias_wide = lax.all_gather(bias_terms, ("x", "core"), axis=0, tiled=True)
    cores, chips = lax.axis_size("core"), lax.axis_size("x")
    my_core, my_chip = lax.axis_index("core"), lax.axis_index("x")
    shard_units = hidden_units // (cores * chips)
    own_start = my_field * own_units
    own_bias = lax.dynamic_slice(bias_wide.reshape(-1, 1), (own_start, 0), (own_units, 1))
    own_grad = own_columns(
        grad_act,
        own_start // shard_units,
        own_start % shard_units // own_units,
        own_units,
        shard_units,
    )
    own_grad = lax.optimization_barrier(own_grad.astype(f32))
    slot_row = (jnp.arange(fields * half, dtype=jnp.int32) // half)[:, None]
    weight_pairs = weight_turned.T
    below = jnp.pad(weight_pairs, ((0, half), (0, 0)))
    above = jnp.pad(weight_pairs, ((half, 0), (0, 0)))
    weight_rows = lax.optimization_barrier(
        row_major(
            jnp.where(slot_row < my_field, below, jnp.where(slot_row > my_field, above, 0))
        )
    )

    preact = jnp.sum(shares.astype(f32), 0) + own_bias.astype(f32)
    gate_value = jax.nn.sigmoid(preact)
    own_slope = (
        own_grad * gate_value * (1.0 + preact * (1.0 - gate_value))
    ).astype(bf16)
    slope_turned = exchange(
        jnp.broadcast_to(own_slope[None], (fields, own_units, sample_rows))
    ).reshape(hidden_units, sample_rows)

    pair_grad = lax.optimization_barrier(
        jnp.dot(weight_rows, slope_turned, preferred_element_type=f32).astype(bf16)
    )
    pair_grad = pair_grad.reshape(fields, half, sample_rows).astype(f32)
    outgoing = (pair_grad * mine_wide).astype(bf16)
    returned = exchange(outgoing).astype(f32)

    halves = slope_turned.reshape(chips, cores, shard_units, sample_rows)
    kept = lax.dynamic_index_in_dim(halves, my_core, 1, keepdims=False)
    got = lax.ppermute(slope_turned, "core", [(0, 1), (1, 0)])
    got = lax.dynamic_index_in_dim(got.reshape(halves.shape), my_core, 1, keepdims=False)
    chip_sum = lax.dot_general(
        kept, pair_rows, (((2,), (1,)), ((), ())), preferred_element_type=f32
    )
    chip_sum = chip_sum + lax.dot_general(
        got, other_rows, (((2,), (1,)), ((), ())), preferred_element_type=f32
    )
    blocks = [
        lax.dynamic_index_in_dim(chip_sum, (my_chip + step) % chips, 0, keepdims=False)
        for step in range(chips)
    ]
    weight_total, *blocks = lax.optimization_barrier(
        (blocks[0], *[block.astype(bf16) for block in blocks[1:]])
    )
    for step, block in enumerate(blocks, 1):
        chip_got = lax.ppermute(
            block, "x", [(i, (i + step) % chips) for i in range(chips)]
        )
        weight_total = weight_total + chip_got.astype(f32)

    local = pair_grad * received_wide
    full = jnp.concatenate(
        [jnp.where(upper, returned, local), jnp.where(upper, local, returned)], 1
    )
    full = full / jnp.sqrt(counts[:, 0].astype(f32))[None, None, :]
    turned = row_major(full.astype(bf16).reshape(fields * depth, sample_rows))
    entry_grad = turned.T[:, None, :]
    return entry_grad, weight_total.T[None]


def solution(mesh):
    fields = mesh.shape["field"]
    split = Mesh(
        mesh.devices.reshape(fields, mesh.shape["batch"] // 2, 2), ("field", "x", "core")
    )
    batch = ("x", "core")
    in_specs = (
        P(batch, "field", None),
        P(batch, "field"),
        P("field", None, batch),
        P(batch),
        P(batch, None),
    )
    out_specs = (P(batch, "field", None), P("field", None, batch))
    return jax.shard_map(body, mesh=split, in_specs=in_specs, out_specs=out_specs, check_vma=False)
```

```python
import jax
import jax.numpy as jnp
from jax import lax
from jax.experimental.layout import Layout, with_layout_constraint
from jax.experimental import pallas as pl
from jax.experimental.pallas import tpu as pltpu
from jax.sharding import Mesh
from jax.sharding import PartitionSpec as P

f32, bf16 = jnp.float32, jnp.bfloat16


def row_major(array):
    return with_layout_constraint(array, Layout(major_to_minor=tuple(range(array.ndim))))


def exchange(blocks):
    return lax.all_to_all(blocks, "field", split_axis=0, concat_axis=0, tiled=True)


def grad_kernel(place_ref, grad_ref, own_ref, turned_ref):
    turned_ref[...] = grad_ref[...].astype(f32).T
    rows = own_ref.shape[0]
    start = pl.multiple_of(place_ref[1] * rows, rows)
    own_ref[...] = turned_ref[pl.ds(start, rows), :].astype(bf16)


def own_columns(grad_act, shard, place, units, shard_units):
    samples = grad_act.shape[0]
    return pl.pallas_call(
        grad_kernel,
        grid_spec=pltpu.PrefetchScalarGridSpec(
            num_scalar_prefetch=1,
            grid=(1,),
            in_specs=[pl.BlockSpec((samples, shard_units), lambda i, place: (0, place[0]))],
            out_specs=pl.BlockSpec((units, samples), lambda i, place: (0, 0)),
            scratch_shapes=[pltpu.VMEM((shard_units, samples), f32)],
        ),
        out_shape=jax.ShapeDtypeStruct((units, samples), bf16),
        name="owngrad",
    )(jnp.stack([shard, place]).astype(jnp.int32), grad_act)


def body(pooled, counts, w_pairs, bias_terms, grad_act):
    sample_rows = pooled.shape[0]
    fields = lax.axis_size("field")
    depth = pooled.shape[2] // fields
    half = depth // 2
    hidden_units = grad_act.shape[1]
    pair_count = w_pairs.shape[1]
    own_units = hidden_units // fields
    my_field = lax.axis_index("field")

    embedded = pooled.reshape(sample_rows, fields, depth).transpose(1, 2, 0)
    partner = jnp.arange(fields, dtype=jnp.int32)[:, None, None]
    upper = partner < my_field
    mine = jnp.where(upper, embedded[:, half:], embedded[:, :half])
    outbound = jnp.where(upper, embedded[:, :half], embedded[:, half:])
    received = exchange(outbound)
    weight_turned = row_major(
        lax.all_gather(row_major(w_pairs[0].T), ("x", "core"), axis=0, tiled=True)
    )

    received_wide, mine_wide = received.astype(f32), mine.astype(f32)
    products = (mine_wide * received_wide).astype(bf16)
    slot = jnp.arange(fields - 1, dtype=jnp.int32)[:, None, None]
    pair_rows = jnp.where(slot >= my_field, products[1:], products[:-1])
    pair_rows = pair_rows.reshape(pair_count, sample_rows)

    partial_hidden = jnp.dot(weight_turned, pair_rows, preferred_element_type=f32)
    partial_hidden = row_major(partial_hidden.astype(bf16))
    shares = exchange(partial_hidden.reshape(fields, own_units, sample_rows))
    other_rows = lax.ppermute(pair_rows, "core", [(0, 1), (1, 0)])

    bias_wide = lax.all_gather(bias_terms, ("x", "core"), axis=0, tiled=True)
    cores, chips = lax.axis_size("core"), lax.axis_size("x")
    my_core, my_chip = lax.axis_index("core"), lax.axis_index("x")
    shard_units = hidden_units // (cores * chips)
    own_start = my_field * own_units
    own_bias = lax.dynamic_slice(bias_wide.reshape(-1, 1), (own_start, 0), (own_units, 1))
    own_grad = own_columns(
        grad_act,
        own_start // shard_units,
        own_start % shard_units // own_units,
        own_units,
        shard_units,
    )
    own_grad = lax.optimization_barrier(own_grad.astype(f32))
    slot_row = (jnp.arange(fields * half, dtype=jnp.int32) // half)[:, None]
    weight_pairs = weight_turned.T
    below = jnp.pad(weight_pairs, ((0, half), (0, 0)))
    above = jnp.pad(weight_pairs, ((half, 0), (0, 0)))
    weight_rows = lax.optimization_barrier(
        row_major(
            jnp.where(slot_row < my_field, below, jnp.where(slot_row > my_field, above, 0))
        )
    )

    preact = jnp.sum(shares.astype(f32), 0) + own_bias.astype(f32)
    gate_value = jax.nn.sigmoid(preact)
    own_slope = (
        own_grad * gate_value * (1.0 + preact * (1.0 - gate_value))
    ).astype(bf16)
    slope_turned = exchange(
        jnp.broadcast_to(own_slope[None], (fields, own_units, sample_rows))
    ).reshape(hidden_units, sample_rows)

    pair_grad = lax.optimization_barrier(
        jnp.dot(weight_rows, slope_turned, preferred_element_type=f32).astype(bf16)
    )
    pair_grad = pair_grad.reshape(fields, half, sample_rows).astype(f32)
    outgoing = (pair_grad * mine_wide).astype(bf16)
    returned = exchange(outgoing).astype(f32)

    halves = slope_turned.reshape(chips, cores, shard_units, sample_rows)
    kept = lax.dynamic_index_in_dim(halves, my_core, 1, keepdims=False)
    got = lax.ppermute(slope_turned, "core", [(0, 1), (1, 0)])
    got = lax.dynamic_index_in_dim(got.reshape(halves.shape), my_core, 1, keepdims=False)
    chip_sum = lax.dot_general(
        kept, pair_rows, (((2,), (1,)), ((), ())), preferred_element_type=f32
    )
    chip_sum = chip_sum + lax.dot_general(
        got, other_rows, (((2,), (1,)), ((), ())), preferred_element_type=f32
    )
    blocks = [
        lax.dynamic_index_in_dim(chip_sum, (my_chip + step) % chips, 0, keepdims=False)
        for step in range(chips)
    ]
    weight_total, *blocks = lax.optimization_barrier(
        (blocks[0], *[block.astype(bf16) for block in blocks[1:]])
    )
    for step, block in enumerate(blocks, 1):
        chip_got = lax.ppermute(
            block, "x", [(i, (i + step) % chips) for i in range(chips)]
        )
        weight_total = weight_total + chip_got.astype(f32)

    root = jnp.sqrt(counts[:, 0].astype(f32))[None, None, :]
    late_grad, _ = lax.optimization_barrier((pair_grad.astype(bf16), outgoing))
    local = lax.optimization_barrier((late_grad.astype(f32) * received_wide / root).astype(bf16))
    returned = (returned / root).astype(bf16)
    full = jnp.concatenate(
        [jnp.where(upper, returned, local), jnp.where(upper, local, returned)], 1
    )
    turned = row_major(full.reshape(fields * depth, sample_rows))
    entry_grad = turned.T[:, None, :]
    return entry_grad, weight_total.T[None]


def solution(mesh):
    fields = mesh.shape["field"]
    split = Mesh(
        mesh.devices.reshape(fields, mesh.shape["batch"] // 2, 2), ("field", "x", "core")
    )
    batch = ("x", "core")
    in_specs = (
        P(batch, "field", None),
        P(batch, "field"),
        P("field", None, batch),
        P(batch),
        P(batch, None),
    )
    out_specs = (P(batch, "field", None), P("field", None, batch))
    return jax.shard_map(body, mesh=split, in_specs=in_specs, out_specs=out_specs, check_vma=False)
```
